32 devices in a mesh: grp: 1, tok: 32 (over z, y, x, core).
Axes of the slice: x: 2, y: 2, z: 4, core: 2. Of those that a mesh axis runs over, the one named last changes fastest.
Arguments:
- queries: bfloat16 [4096, 2048], P(('grp', 'tok')), may hold values from -16 to 16
- keys: bfloat16 [4096, 2048], P(('grp', 'tok')), may hold values from -16 to 16
- values: bfloat16 [4096, 2048], P(('grp', 'tok')), may hold values from -6 to 6
- segment: int32 [4096], P(('grp', 'tok')), may hold values from 0 to 41, never falling along the last dimension, each value on 1 to 256 neighbouring positions
- rates: float32 [4096, 2], P(('grp', 'tok')), may hold values from 0.00046875 to 0.0046875
- fast_one: bfloat16 [2048, 512], P(('grp', 'tok')), may hold values from -0.1875 to 0.1875
- fast_three: bfloat16 [2048, 512], P(('grp', 'tok')), may hold values from -0.1875 to 0.1875
- fast_two: bfloat16 [2048, 512], P(('grp', 'tok')), may hold values from -0.25 to 0.25
Outputs:
- attended: bfloat16 [4096, 2048], P(('grp', 'tok'))
- fast_out: bfloat16 [4096, 2048], P(('grp', 'tok'))
The draws below stay inside these ranges and needn't reach their ends.
Inputs may be any that keep to these rules, and one draw needn't show every extreme that they name: `segment`: exemplar numbers never fall along the tokens; each exemplar covers 1 to 256 consecutive tokens.
All inputs are finite; a program needn't handle non-finite values.
Results may differ from the reference program's by a relative error of at most 0.0084.
Values may be sent and summed in bfloat16 or wider, within the bound.
No kernel may reach another device: no remote copies, remote signals or barrier semaphores. Data moves between devices by JAX's collectives and lax.ppermute only.
A program may use at most 128 MiB of HBM per device.

```python
import math
import jax
import jax.numpy as jnp
import numpy as np
from jax import lax

D = 2048
ATT_HEADS = 16
FAST_HEADS = 2
FAST_DIM = 1024
FAST_HID = 512
WINDOW = 128
TOKENS = 4096
SEGS = 42
SEG_MOST = 256


def paired_rows(key):
    base = jax.random.fold_in(key, 7)
    key_q, key_k = jax.random.split(base, 2)
    queries = jnp.clip(jax.random.normal(key_q, (TOKENS, D), jnp.float32), -6.0, 6.0)
    keys = jnp.clip(jax.random.normal(key_k, (TOKENS, D), jnp.float32), -6.0, 6.0)
    return (queries, keys)


def draw_queries(key, part):
    return paired_rows(key)[0].astype(jnp.bfloat16)


def draw_keys(key, part):
    return paired_rows(key)[1].astype(jnp.bfloat16)


def shard_levels(key, extent, shards, least, high):
    factor_of, own = 1.0, jax.random.fold_in(key, 6)
    for dim, blocks in shards:
        steps = jnp.exp(jax.random.uniform(jax.random.fold_in(own, dim), (blocks,), jnp.float32, least / len(shards), high / len(shards)))
        factor_of = factor_of * jnp.repeat(steps, extent[dim] // blocks).reshape([-1 if axis == dim else 1 for axis in range(len(extent))])
    return factor_of


def profile(amount, total, bound, skew):
    portions = [(1 << 20) // math.isqrt(standing ** skew) + 1 for standing in range(2, amount + 1)]
    rest, given = total - bound - (amount - 1), [1] * (amount - 1)
    while rest > 0:
        candidates = [i for i in range(amount - 1) if given[i] < bound]
        whole, left = sum([portions[i] for i in candidates]), rest
        for i in candidates:
            extra = min(bound - given[i], max(1, left * portions[i] // whole), rest)
            given[i] = given[i] + extra
            rest = rest - extra
    return np.array([bound] + given)


def ragged_sizes(rng, amount, total, reach, skew):
    if amount == 2:
        one = jax.random.randint(rng, (), max(1, total - reach), min(reach, total - 1) + 1)
        return jnp.stack([one, total - one])
    tallies = jnp.asarray(profile(amount, total, reach, skew), jnp.int32)
    couples = (amount - 1) // 2
    donor, taker = tallies[1:1 + 2 * couples:2], tallies[2:2 + 2 * couples:2]
    room = jnp.minimum(donor - 1, reach - taker)
    moved = jax.random.randint(jax.random.fold_in(rng, 1), (couples,), 0, 1 << 20) % (room + 1)
    tallies = tallies.at[1:1 + 2 * couples:2].set(donor - moved).at[2:2 + 2 * couples:2].set(taker + moved)
    return tallies[jax.random.permutation(jax.random.fold_in(rng, 2), amount)]


def noise(stream_key, shape, scale, reach, cuts=(), kind=jnp.bfloat16):
    entries = jax.random.normal(stream_key, shape, jnp.float32) * scale
    if len(cuts) > 0:
        entries = shard_levels(stream_key, shape, cuts, -0.22, 0.18) * entries
    return jnp.clip(entries, min=-reach, max=reach).astype(kind)


def setup_inputs(seed: int = 0, part: int = 0) -> dict:
    key_list = jax.random.split(jax.random.key(seed), 9)
    part_splits = jax.random.split(jax.random.fold_in(key_list[8], part), 9)
    queries = draw_queries(jax.random.fold_in(jax.random.fold_in(key_list[8], part), 71), part)
    keys = draw_keys(jax.random.fold_in(jax.random.fold_in(key_list[8], part), 71), part)
    values = noise(part_splits[2], (TOKENS, D), 1.0, 6.0, ((0, 32),))
    segment = jnp.searchsorted(jnp.cumsum(ragged_sizes(part_splits[3], SEGS, TOKENS, SEG_MOST, 1)), jnp.arange(TOKENS), side="right").astype(jnp.int32)
    rates = jnp.clip(jnp.exp(math.log(0.0046875) - 2.3025852 * jax.random.uniform(part_splits[4], (TOKENS, FAST_HEADS), jnp.float32) ** shard_levels(part_splits[4], (TOKENS, FAST_HEADS), ((0, 32),), -0.2, 0.2)), 0.00046875, 0.0046875)
    fast_one = noise(part_splits[5], (FAST_HEADS * FAST_DIM, FAST_HID), FAST_DIM ** -0.5, 0.1875, ((0, 32),))
    fast_three = noise(part_splits[6], (FAST_HEADS * FAST_DIM, FAST_HID), FAST_DIM ** -0.5, 0.1875, ((0, 32),))
    fast_two = noise(part_splits[7], (FAST_HEADS * FAST_DIM, FAST_HID), FAST_HID ** -0.5, 0.25, ((0, 32),))
    return dict(queries=queries, keys=keys, values=values, segment=segment, rates=rates, fast_one=fast_one, fast_three=fast_three, fast_two=fast_two)


EPS = 1e-06

def attend(queries, keys, values, segment):
    head_dim = D // ATT_HEADS
    scale = 1.0 / math.sqrt(head_dim)
    blocks = queries.shape[0] // WINDOW
    pad_keys = jnp.concatenate([jnp.zeros((WINDOW, D), keys.dtype), keys], 0)
    pad_values = jnp.concatenate([jnp.zeros((WINDOW, D), values.dtype), values], 0)
    pad_seg = jnp.concatenate([jnp.full((WINDOW,), -1, jnp.int32), segment.astype(jnp.int32)], 0)

    def one_block(index):
        start = (index * WINDOW).astype(jnp.int32)
        q_blk = lax.dynamic_slice_in_dim(queries, start, WINDOW, 0)
        k_blk = lax.dynamic_slice_in_dim(pad_keys, start, 2 * WINDOW, 0)
        v_blk = lax.dynamic_slice_in_dim(pad_values, start, 2 * WINDOW, 0)
        s_blk = lax.dynamic_slice_in_dim(pad_seg, start, 2 * WINDOW, 0)
        s_own = lax.dynamic_slice_in_dim(segment.astype(jnp.int32), start, WINDOW, 0)
        qh = q_blk.reshape(WINDOW, ATT_HEADS, head_dim).astype(jnp.float32)
        kh = k_blk.reshape(2 * WINDOW, ATT_HEADS, head_dim).astype(jnp.float32)
        vh = v_blk.reshape(2 * WINDOW, ATT_HEADS, head_dim).astype(jnp.float32)
        scores = jnp.einsum('qhd,khd->hqk', qh, kh) * scale
        rows = jnp.arange(WINDOW, dtype=jnp.int32)[:, None] + WINDOW
        cols = jnp.arange(2 * WINDOW, dtype=jnp.int32)[None, :]
        allowed = (cols <= rows) & (rows - cols < WINDOW) & (s_blk[None, :] == s_own[:, None])
        masked = jnp.where(allowed[None], scores, jnp.float32(-1e+30))
        top = lax.optimization_barrier(jnp.max(masked, axis=2, keepdims=True))
        expo = jnp.where(allowed[None], jnp.exp(masked - top), jnp.float32(0.0))
        probs = (expo / lax.optimization_barrier(jnp.sum(expo, axis=2, keepdims=True))).astype(jnp.bfloat16)
        out = jnp.einsum('hqk,khd->qhd', probs.astype(jnp.float32), vh)
        return out.reshape(WINDOW, D).astype(jnp.bfloat16)
    outs = lax.map(one_block, jnp.arange(blocks, dtype=jnp.int32))
    return outs.reshape(blocks * WINDOW, D)

def heads_apply(rows, weight):
    grouped = rows.reshape(rows.shape[0], FAST_HEADS, FAST_DIM).astype(jnp.float32)
    matrix = weight.reshape(FAST_HEADS, FAST_DIM, FAST_HID).astype(jnp.float32)
    return jnp.einsum('thd,hdc->thc', grouped, matrix)

def outer_sum(rows, hidden):
    grouped = rows.reshape(rows.shape[0], FAST_HEADS, FAST_DIM).astype(jnp.float32)
    return jnp.einsum('thd,thc->hdc', grouped, hidden.astype(jnp.float32))

def renorm(weight, grad):
    matrix = weight.reshape(FAST_HEADS, FAST_DIM, FAST_HID).astype(jnp.float32)
    update = matrix - grad
    old_len = jnp.sqrt(lax.optimization_barrier(jnp.sum(matrix * matrix, axis=1)))
    new_len = jnp.sqrt(lax.optimization_barrier(jnp.sum(update * update, axis=1)) + EPS)
    return (update * (old_len / new_len)[:, None, :]).astype(jnp.bfloat16)

def reference(queries, keys, values, segment, rates, fast_one, fast_three, fast_two):
    attended = attend(queries, keys, values, segment)
    width = FAST_HEADS * FAST_DIM
    key_fast = keys[:, :width]
    value_fast = values[:, :width]
    query_fast = queries[:, :width]
    rate = rates.astype(jnp.float32)[:, :, None]
    a_one = heads_apply(key_fast, fast_one)
    a_three = heads_apply(key_fast, fast_three)
    sig = jax.nn.sigmoid(a_one)
    weighted = (-rate * a_one * sig * a_three).astype(jnp.bfloat16)
    grad_two = outer_sum(value_fast, weighted)
    back = -rate * heads_apply(value_fast, fast_two)
    delta_one = (back * a_three * sig * (1.0 + a_one * (1.0 - sig))).astype(jnp.bfloat16)
    delta_three = (back * a_one * sig).astype(jnp.bfloat16)
    grad_one = outer_sum(key_fast, delta_one)
    grad_three = outer_sum(key_fast, delta_three)
    new_one = renorm(fast_one, grad_one)
    new_three = renorm(fast_three, grad_three)
    new_two = renorm(fast_two, grad_two)
    grouped = query_fast.reshape(query_fast.shape[0], FAST_HEADS, FAST_DIM).astype(jnp.float32)
    b_one = jnp.einsum('thd,hdc->thc', grouped, new_one.astype(jnp.float32))
    b_three = jnp.einsum('thd,hdc->thc', grouped, new_three.astype(jnp.float32))
    mixed = (jax.nn.silu(b_one) * b_three).astype(jnp.bfloat16)
    fast_out = jnp.einsum('thc,hdc->thd', mixed.astype(jnp.float32), new_two.astype(jnp.float32))
    fast_out = fast_out.reshape(query_fast.shape[0], width).astype(jnp.bfloat16)
    return (attended, fast_out)
```

```python
import functools
import math

import jax
import jax.numpy as jnp
from jax import lax
from jax.experimental import pallas as pl
from jax.experimental.pallas import tpu as pltpu
from jax.sharding import PartitionSpec as P

ATT_HEADS = 16
FAST_HEADS = 2
EPS = 1e-06


BF = jnp.bfloat16
F32 = jnp.float32
VM = pl.BlockSpec(memory_space=pltpu.VMEM)
SM = pl.BlockSpec(memory_space=pltpu.SMEM)
ANY = pl.BlockSpec(memory_space=pl.ANY)


def struct(shape, dtype):
    return jax.ShapeDtypeStruct(shape, dtype)


def call(body, outs, in_specs, out_specs, args, scratch=(), flops=0, name=None):
    moved = sum(a.size * a.dtype.itemsize for a in args)
    moved += sum(math.prod(o.shape) * jnp.dtype(o.dtype).itemsize for o in outs)
    return pl.pallas_call(
        body,
        out_shape=tuple(outs),
        in_specs=in_specs,
        out_specs=tuple(out_specs),
        scratch_shapes=list(scratch),
        cost_estimate=pl.CostEstimate(flops=flops, bytes_accessed=moved, transcendentals=0),
        compiler_params=pltpu.CompilerParams(vmem_limit_bytes=48 << 20),
        name=name,
    )(*args)


def swap(value, offset):
    count = lax.axis_size("tok")
    return lax.ppermute(value, "tok", [(i, i ^ offset) for i in range(count)])


def nn(a, b):
    return lax.dot_general(a, b, (((1,), (0,)), ((), ())), preferred_element_type=F32)


def nt(a, b):
    return lax.dot_general(a, b, (((1,), (1,)), ((), ())), preferred_element_type=F32)


def tn(a, b):
    return lax.dot_general(a, b, (((0,), (0,)), ((), ())), preferred_element_type=F32)


def prep_kernel(half, me_ref, k_ref, v_ref, r_ref, w1_ref, w3_ref, w2_ref, *outs):
    kv_ref, ko_ref, vo_ref = outs[:3]
    pieces = outs[3:]
    me = me_ref[0]
    dim = ko_ref.shape[1]
    head = me // half
    quarter = me % 4
    mine = pl.ds(pl.multiple_of(head * dim, dim), dim)
    other = pl.ds(pl.multiple_of((1 - head) * dim, dim), dim)
    ko_ref[...] = k_ref[:, other]
    kv_ref[0] = k_ref[:, mine]
    rate0, rate1 = r_ref[:, 0:1], r_ref[:, 1:2]
    own = jnp.where(head == 0, rate0, rate1)
    far = jnp.where(head == 0, rate1, rate0)
    vo_ref[...] = (-far * v_ref[:, other].astype(F32)).astype(BF)
    kv_ref[1] = (-own * v_ref[:, mine].astype(F32)).astype(BF)
    wide = pieces[0].shape[2]
    for k in range(4):
        cols = pl.ds(pl.multiple_of((quarter ^ k) * wide, wide), wide)
        for m, w_ref in enumerate((w1_ref, w3_ref, w2_ref)):
            pieces[k][m] = w_ref[:, cols]


def query_kernel(half, me_ref, q_ref, qm_ref, qo_ref):
    dim = qm_ref.shape[1]
    head = me_ref[0] // half
    qm_ref[...] = q_ref[:, pl.ds(pl.multiple_of(head * dim, dim), dim)]
    qo_ref[...] = q_ref[:, pl.ds(pl.multiple_of((1 - head) * dim, dim), dim)]


def attention_kernel(heads, me_ref, q_ref, k_ref, v_ref, pk_ref, pv_ref, sc_ref, sr_ref, ps_ref, o_ref):
    count, width = q_ref.shape
    dim = width // heads
    scale = 1.0 / math.sqrt(dim)
    rows = lax.broadcasted_iota(jnp.int32, (count, count), 0)
    cols = lax.broadcasted_iota(jnp.int32, (count, count), 1)
    here = (cols <= rows) & (sc_ref[...] == sr_ref[...])
    before = (cols > rows) & (sc_ref[...] == ps_ref[...]) & (me_ref[0] > 0)
    for h in range(heads):
        part = slice(h * dim, (h + 1) * dim)
        q = q_ref[:, part]
        s0 = jnp.where(before, nt(q, pk_ref[:, part]) * scale, F32(-1e30))
        s1 = jnp.where(here, nt(q, k_ref[:, part]) * scale, F32(-1e30))
        top = jnp.maximum(jnp.max(s0, axis=1, keepdims=True), jnp.max(s1, axis=1, keepdims=True))
        e0 = jnp.where(before, jnp.exp(s0 - top), F32(0.0))
        e1 = jnp.where(here, jnp.exp(s1 - top), F32(0.0))
        total = jnp.sum(e0, axis=1, keepdims=True) + jnp.sum(e1, axis=1, keepdims=True)
        out = nn((e0 / total).astype(BF), pv_ref[:, part]) + nn((e1 / total).astype(BF), v_ref[:, part])
        o_ref[:, part] = out.astype(BF)


def fetch(sources, held, sems):
    copies = []
    for i, source in enumerate(sources):
        size = source.shape[0]
        copies.append(pltpu.make_async_copy(source, held.at[pl.ds(i * size, size)], sems.at[i]))
        copies[-1].start()
    return copies


def forward_kernel(half, group, me_ref, *refs):
    own, own_c, x1, x1_c, z, z_c, x2, x2_c = refs[:8]
    bundles = refs[8 : 8 + group]
    s_ref, e1_ref, e3_ref, w2_ref, wt_ref, held, w13, sems = refs[8 + group :]
    copies = fetch([own.at[0], own_c.at[0], x1.at[0], x1_c.at[0], z, z_c, x2, x2_c], held, sems)
    me = me_ref[0]
    quarter, place = me % 4, (me // 4) % group
    wide = w2_ref.shape[1]
    rows = bundles[0].shape[2]
    for j in range(group):
        for k in range(4):
            at = pl.ds(pl.multiple_of(((place ^ j) * 4 + (quarter ^ k)) * rows, rows), rows)
            w13[at, 0:wide] = bundles[j][k, 0]
            w13[at, wide : 2 * wide] = bundles[j][k, 1]
            w2_ref[at, :] = bundles[j][k, 2]
    share = wt_ref.shape[1]
    pick = lax.broadcasted_iota(jnp.int32, (share, wide), 1) == (
        lax.broadcasted_iota(jnp.int32, (share, wide), 0) + place * share
    )
    pick = pick.astype(F32).astype(BF)
    wt_ref[0] = nt(pick, w13[:, 0:wide])
    wt_ref[1] = nt(pick, w13[:, wide : 2 * wide])
    wt_ref[2] = nt(pick, w2_ref[...])
    for copy in copies:
        copy.wait()
    both = nn(held[...], w13[...])
    a1, a3 = both[:, :wide], both[:, wide:]
    sig = jax.nn.sigmoid(a1)
    s_ref[...] = (a1 * sig * a3).astype(BF)
    e1_ref[...] = a3 * sig * (1.0 + a1 * (1.0 - sig))
    e3_ref[...] = a1 * sig


def backward_kernel(group, me_ref, *refs):
    own, own_c, x1, x1_c = refs[:4]
    kz, kz_c, kx2, kx2_c, vz, vz_c, vx2, vx2_c = refs[4:12]
    s_ref, e1_ref, e3_ref, w2_ref = refs[12:16]
    outs = refs[16 : 16 + group]
    keys, values, delta, grads, ksems, vsems = refs[16 + group :]
    kcopies = fetch([own.at[0], own_c.at[0], x1.at[0], x1_c.at[0], kz, kz_c, kx2, kx2_c], keys, ksems)
    vcopies = fetch([own.at[1], own_c.at[1], x1.at[1], x1_c.at[1], vz, vz_c, vx2, vx2_c], values, vsems)
    place = (me_ref[0] // 4) % group
    wide = w2_ref.shape[1]
    for copy in vcopies:
        copy.wait()
    back = nn(values[...], w2_ref[...])
    delta[:, 0:wide] = (back * e1_ref[...]).astype(BF)
    delta[:, wide : 2 * wide] = (back * e3_ref[...]).astype(BF)
    grads[pl.ds(2 * wide, wide)] = tn(s_ref[...], values[...])
    for copy in kcopies:
        copy.wait()
    grads[pl.ds(0, 2 * wide)] = tn(delta[...], keys[...])
    share = outs[0].shape[1]
    for j in range(group):
        for m in range(3):
            at = pl.ds(pl.multiple_of(m * wide + (place ^ j) * share, share), share)
            outs[j][m] = grads[at, :].astype(outs[j].dtype)


def update_kernel(group, wt_ref, *refs):
    parts, out_ref = refs[:group], refs[group]
    grad = parts[0][...].astype(F32)
    for part in parts[1:]:
        grad = grad + part[...].astype(F32)
    weight = wt_ref[...]
    fresh = weight - grad
    old_len = jnp.sqrt(jnp.sum(weight * weight, axis=2, keepdims=True))
    new_len = jnp.sqrt(jnp.sum(fresh * fresh, axis=2, keepdims=True) + EPS)
    out_ref[...] = (fresh * (old_len / new_len)).astype(BF)


def output_kernel(parts, *refs):
    qm, qz, cm, cz = refs[:4]
    shares = refs[4 : 4 + parts]
    own_ref, send_ref, held, fresh, sems = refs[4 + parts :]
    copies = fetch([qm, qz, cm, cz], held, sems)
    share = shares[0].shape[1]
    wide = share * parts
    for i in range(parts):
        for m in range(3):
            fresh[pl.ds(m * wide + i * share, share)] = shares[i][m].astype(fresh.dtype)
    for copy in copies:
        copy.wait()
    both = nt(held[...], fresh[pl.ds(0, 2 * wide)].astype(BF))
    gate = both[:, :wide]
    mixed = (gate * jax.nn.sigmoid(gate) * both[:, wide:]).astype(BF)
    out = nn(mixed, fresh[pl.ds(2 * wide, wide)].astype(BF))
    rows = own_ref.shape[0]
    own_ref[...] = out[:rows]
    send_ref[...] = out[rows:].astype(BF)


def per_device(queries, keys, values, segment, rates, fast_one, fast_three, fast_two):
    n = lax.axis_size("tok")
    half, group = n // 2, n // 8
    count, width = queries.shape
    dim = width // FAST_HEADS
    rows, hidden = fast_one.shape
    wide = hidden // 4
    share = wide // group
    tokens = 8 * count
    shard = lax.axis_index("tok")
    me = shard.astype(jnp.int32).reshape(1)

    outs = [struct((2, count, dim), BF), struct((count, dim), BF), struct((count, dim), BF)]
    outs += [struct((3, rows, wide), BF)] * 4
    kv, k_other, v_other, *pieces = call(
        functools.partial(prep_kernel, half), outs, [SM] + [VM] * 6, [VM] * 7,
        (me, keys, values, rates, fast_one, fast_three, fast_two), name="prep")
    kz = swap(k_other, half)
    got = [pieces[0]] + [swap(pieces[k], k) for k in range(1, 4)]
    kv_x1 = swap(kv, 2)
    kv_c = swap(kv, 1)
    vz = swap(v_other, half)
    bundle = jnp.stack(got)
    bundles = [bundle] + [swap(bundle, 4 * j) for j in range(1, group)]
    kx2 = swap(kz, 2)
    kz_c = swap(kz, 1)
    kv_x1c = swap(kv_x1, 1)
    kx2_c = swap(kx2, 1)
    s, e1, e3, w2, wt = call(
        functools.partial(forward_kernel, half, group),
        [struct((tokens, wide), BF), struct((tokens, wide), F32), struct((tokens, wide), F32),
         struct((dim, wide), BF), struct((3, share, dim), F32)],
        [SM] + [ANY] * 8 + [VM] * group, [VM] * 5,
        (me, kv, kv_c, kv_x1, kv_x1c, kz, kz_c, kx2, kx2_c, *bundles),
        [pltpu.VMEM((tokens, dim), BF), pltpu.VMEM((dim, 2 * wide), BF), pltpu.SemaphoreType.DMA((8,))],
        flops=4 * tokens * dim * wide, name="forward")
    vx2 = swap(vz, 2)
    vz_c = swap(vz, 1)
    vx2_c = swap(vx2, 1)
    grads = call(
        functools.partial(backward_kernel, group),
        [struct((3, share, dim), F32)] + [struct((3, share, dim), BF)] * (group - 1),
        [SM] + [ANY] * 12 + [VM] * 4, [VM] * group,
        (me, kv, kv_c, kv_x1, kv_x1c, kz, kz_c, kx2, kx2_c, vz, vz_c, vx2, vx2_c, s, e1, e3, w2),
        [pltpu.VMEM((tokens, dim), BF), pltpu.VMEM((tokens, dim), BF), pltpu.VMEM((tokens, 2 * wide), BF),
         pltpu.VMEM((3 * wide, dim), F32), pltpu.SemaphoreType.DMA((8,)), pltpu.SemaphoreType.DMA((8,))],
        flops=8 * tokens * dim * wide, name="backward")
    sums = [grads[0]] + [swap(grads[j], 4 * j) for j in range(1, group)]
    (fresh,) = call(functools.partial(update_kernel, group), [struct((3, share, dim), BF)],
                    [VM] * (group + 1), [VM], (wt, *sums), name="update")

    q_mine, q_other = call(functools.partial(query_kernel, half), [struct((count, dim), BF)] * 2,
                           [SM, VM], [VM] * 2, (me, queries), name="query")
    qz = swap(q_other, half)
    q_c = swap(q_mine, 1)
    qz_c = swap(qz, 1)

    parts = 2 * group
    shares = [fresh] + [swap(fresh, 2 * j) for j in range(1, parts)]
    kind = BF if share % 16 == 0 else F32
    own, send = call(
        functools.partial(output_kernel, parts),
        [struct((2 * count, dim), F32), struct((2 * count, dim), BF)],
        [ANY] * 4 + [VM] * parts, [VM] * 2, (q_mine, qz, q_c, qz_c, *shares),
        [pltpu.VMEM((4 * count, dim), BF), pltpu.VMEM((3 * parts * share, dim), kind), pltpu.SemaphoreType.DMA((4,))],
        flops=6 * 4 * count * dim * parts * share, name="output")
    total = (own + swap(send, 1).astype(F32)).astype(BF)
    away = swap(total[count:], half)
    here = total[:count]
    head = shard // half
    fast_out = jnp.where(head == 0, jnp.concatenate([here, away], 1), jnp.concatenate([away, here], 1))

    chain = [(i, i + 1) for i in range(n - 1)]
    pk = lax.ppermute(keys, "tok", chain)
    pv = lax.ppermute(values, "tok", chain)
    seg_row = segment.reshape(1, count)
    ps = lax.ppermute(seg_row, "tok", chain)
    (attended,) = call(
        functools.partial(attention_kernel, ATT_HEADS), [struct((count, width), BF)],
        [SM] + [VM] * 8, [VM],
        (me, queries, keys, values, pk, pv, segment.reshape(count, 1), seg_row, ps),
        flops=8 * count * count * width, name="attention")
    return attended, fast_out


def solution(mesh):
    placed = tuple(P(("grp", "tok")) if i == 3 else P(("grp", "tok"), None) for i in range(8))
    return jax.shard_map(
        per_device,
        mesh=mesh,
        in_specs=placed,
        out_specs=(P(("grp", "tok"), None), P(("grp", "tok"), None)),
        check_vma=False,
    )
```

```python
import functools
import math

import jax
import jax.numpy as jnp
from jax import lax
from jax.experimental import pallas as pl
from jax.experimental.pallas import tpu as pltpu
from jax.sharding import PartitionSpec as P


ATT_HEADS = 16
FAST_HEADS = 2
EPS = 1e-06


BF = jnp.bfloat16
F32 = jnp.float32
VM = pl.BlockSpec(memory_space=pltpu.VMEM)
SM = pl.BlockSpec(memory_space=pltpu.SMEM)
HBM = pl.BlockSpec(memory_space=pltpu.HBM)


def struct(shape, dtype):
    return jax.ShapeDtypeStruct(shape, dtype)


def call(body, outs, in_specs, out_specs, args, scratch=(), flops=0, limit=20):
    moved = sum(a.size * a.dtype.itemsize for a in args)
    moved += sum(math.prod(o.shape) * jnp.dtype(o.dtype).itemsize for o in outs)
    return pl.pallas_call(
        body,
        out_shape=tuple(outs),
        in_specs=in_specs,
        out_specs=tuple(out_specs),
        scratch_shapes=list(scratch),
        cost_estimate=pl.CostEstimate(flops=flops, bytes_accessed=moved, transcendentals=0),
        compiler_params=pltpu.CompilerParams(vmem_limit_bytes=limit << 20),
    )(*args)


def in_hbm(*arrays):
    return [pltpu.with_memory_space_constraint(a, pltpu.HBM) for a in arrays]


def shift(value, pairs):
    return lax.ppermute(value, "tok", pairs)


def swap(value, offset):
    return shift(value, [(i, i ^ offset) for i in range(lax.axis_size("tok"))])


def nn(a, b):
    return lax.dot_general(a, b, (((1,), (0,)), ((), ())), preferred_element_type=F32)


def nt(a, b):
    return lax.dot_general(a, b, (((1,), (1,)), ((), ())), preferred_element_type=F32)


def tn(a, b):
    return lax.dot_general(a, b, (((0,), (0,)), ((), ())), preferred_element_type=F32)


def run(copies):
    for copy in copies:
        copy.start()
    for copy in copies:
        copy.wait()


def first_kernel(half, me_ref, k_ref, w1_ref, w3_ref, w2_ref, ko_ref, *rest):
    pieces, sems = rest[:4], rest[4]
    me = me_ref[0]
    dim = ko_ref.shape[1]
    other = pl.ds(pl.multiple_of((1 - me // half) * dim, dim), dim)
    copies = [pltpu.make_async_copy(k_ref.at[:, other], ko_ref, sems.at[0])]
    wide = pieces[0].shape[2]
    for k in range(4):
        cols = pl.ds(pl.multiple_of((me % 4 ^ k) * wide, wide), wide)
        for m, w_ref in enumerate((w1_ref, w3_ref, w2_ref)):
            copies.append(pltpu.make_async_copy(w_ref.at[:, cols], pieces[k].at[m], sems.at[1 + 3 * k + m]))
    run(copies)


def second_kernel(half, me_ref, k_ref, v_ref, kv_ref, vo_ref, sems):
    head = me_ref[0] // half
    dim = vo_ref.shape[1]
    mine = pl.ds(pl.multiple_of(head * dim, dim), dim)
    other = pl.ds(pl.multiple_of((1 - head) * dim, dim), dim)
    run([
        pltpu.make_async_copy(v_ref.at[:, other], vo_ref, sems.at[0]),
        pltpu.make_async_copy(k_ref.at[:, mine], kv_ref.at[0], sems.at[1]),
        pltpu.make_async_copy(v_ref.at[:, mine], kv_ref.at[1], sems.at[2]),
    ])


def query_kernel(half, me_ref, q_ref, qm_ref, qo_ref, sems):
    head = me_ref[0] // half
    dim = qm_ref.shape[1]
    run([
        pltpu.make_async_copy(q_ref.at[:, pl.ds(pl.multiple_of((1 - head) * dim, dim), dim)], qo_ref, sems.at[0]),
        pltpu.make_async_copy(q_ref.at[:, pl.ds(pl.multiple_of(head * dim, dim), dim)], qm_ref, sems.at[1]),
    ])


def attention_kernel(heads, me_ref, q_ref, k_ref, v_ref, pk_ref, pv_ref, sc_ref, sr_ref, ps_ref, o_ref):
    count, width = q_ref.shape
    dim = width // heads
    scale = 1.0 / math.sqrt(dim)
    rows = lax.broadcasted_iota(jnp.int32, (count, count), 0)
    cols = lax.broadcasted_iota(jnp.int32, (count, count), 1)
    here = (cols <= rows) & (sc_ref[...] == sr_ref[...])
    before = (cols > rows) & (sc_ref[...] == ps_ref[...]) & (me_ref[0] > 0)
    for h in range(heads):
        part = slice(h * dim, (h + 1) * dim)
        q = q_ref[:, part]
        s0 = jnp.where(before, nt(q, pk_ref[:, part]) * scale, F32(-1e30))
        s1 = jnp.where(here, nt(q, k_ref[:, part]) * scale, F32(-1e30))
        top = jnp.maximum(jnp.max(s0, axis=1, keepdims=True), jnp.max(s1, axis=1, keepdims=True))
        e0 = jnp.where(before, jnp.exp(s0 - top), F32(0.0))
        e1 = jnp.where(here, jnp.exp(s1 - top), F32(0.0))
        total = jnp.sum(e0, axis=1, keepdims=True) + jnp.sum(e1, axis=1, keepdims=True)
        out = nn((e0 / total).astype(BF), pv_ref[:, part]) + nn((e1 / total).astype(BF), v_ref[:, part])
        o_ref[:, part] = out.astype(BF)


def rows_of(*parts):
    return jnp.concatenate(parts, 0)


def forward_kernel(half, group, me_ref, r_ref, *refs):
    own, own_c, x1, x1_c, z, z_c, x2, x2_c = refs[:8]
    bundles = refs[8 : 8 + group]
    s_ref, e1_ref, e3_ref, w2_ref, wt_ref, w13 = refs[8 + group :]
    me = me_ref[0]
    quarter, place = me % 4, (me // 4) % group
    wide = w2_ref.shape[1]
    rows = bundles[0].shape[2]
    for j in range(group):
        for k in range(4):
            at = pl.ds(pl.multiple_of(((place ^ j) * 4 + (quarter ^ k)) * rows, rows), rows)
            w13[at, 0:wide] = bundles[j][k, 0]
            w13[at, wide : 2 * wide] = bundles[j][k, 1]
            w2_ref[at, :] = bundles[j][k, 2]
    share = wt_ref.shape[1]
    pick = lax.broadcasted_iota(jnp.int32, (share, wide), 1) == (
        lax.broadcasted_iota(jnp.int32, (share, wide), 0) + place * share
    )
    pick = pick.astype(F32).astype(BF)
    wt_ref[0] = nt(pick, w13[:, 0:wide])
    wt_ref[1] = nt(pick, w13[:, wide : 2 * wide])
    wt_ref[2] = nt(pick, w2_ref[...])
    rate = -jnp.where(me // half == 0, r_ref[:, 0, :], r_ref[:, 1, :]).T
    held = rows_of(own[0], own_c[0], x1[0], x1_c[0], z[...], z_c[...], x2[...], x2_c[...])
    both = nn(held, w13[...])
    count = held.shape[0] // 8
    for i in range(8):
        part = slice(i * count, (i + 1) * count)
        a1, a3 = both[part, :wide], both[part, wide:]
        at = 4 * (i >> 1 & 1) + 2 * (i & 1) + (i >> 2)
        r = rate[:, at : at + 1]
        sig = jax.nn.sigmoid(a1)
        gate = r * a1 * sig
        s_ref[part, :] = (gate * a3).astype(BF)
        e1_ref[part, :] = r * a3 * sig * (1.0 + a1 * (1.0 - sig))
        e3_ref[part, :] = gate


def backward_kernel(group, me_ref, *refs):
    own, own_c, x1, x1_c = refs[:4]
    kz, kz_c, kx2, kx2_c, vz, vz_c, vx2, vx2_c = refs[4:12]
    s_ref, e1_ref, e3_ref, w2_ref = refs[12:16]
    outs = refs[16 : 16 + group]
    (grads,) = refs[16 + group :]
    keys = rows_of(own[0], own_c[0], x1[0], x1_c[0], kz[...], kz_c[...], kx2[...], kx2_c[...])
    values = rows_of(own[1], own_c[1], x1[1], x1_c[1], vz[...], vz_c[...], vx2[...], vx2_c[...])
    place = (me_ref[0] // 4) % group
    wide = w2_ref.shape[1]
    back = nn(values, w2_ref[...])
    delta = jnp.concatenate([(back * e1_ref[...]).astype(BF), (back * e3_ref[...]).astype(BF)], 1)
    grads[pl.ds(2 * wide, wide)] = tn(s_ref[...], values)
    grads[pl.ds(0, 2 * wide)] = tn(delta, keys)
    share = outs[0].shape[1]
    for j in range(group):
        for m in range(3):
            at = pl.ds(pl.multiple_of(m * wide + (place ^ j) * share, share), share)
            outs[j][m] = grads[at, :].astype(outs[j].dtype)


def update_kernel(group, wt_ref, *refs):
    parts, out_ref = refs[:group], refs[group]
    grad = parts[0][...].astype(F32)
    for part in parts[1:]:
        grad = grad + part[...].astype(F32)
    weight = wt_ref[...]
    fresh = weight - grad
    old_len = jnp.sqrt(jnp.sum(weight * weight, axis=2, keepdims=True))
    new_len = jnp.sqrt(jnp.sum(fresh * fresh, axis=2, keepdims=True) + EPS)
    out_ref[...] = (fresh * (old_len / new_len)).astype(BF)


def output_kernel(parts, *refs):
    qm, qz, cm, cz = refs[:4]
    shares = refs[4 : 4 + parts]
    here_ref, away_ref, send_here_ref, send_away_ref, fresh, held = refs[4 + parts :]
    share = shares[0].shape[1]
    wide = share * parts
    for i in range(parts):
        for m in range(3):
            fresh[pl.ds(m * wide + i * share, share)] = shares[i][m].astype(fresh.dtype)
    for i, part in enumerate((qm, qz, cm, cz)):
        held[pl.ds(i * part.shape[0], part.shape[0])] = part[...]
    both = nt(held[...], fresh[pl.ds(0, 2 * wide)].astype(BF))
    gate = both[:, :wide]
    mixed = (gate * jax.nn.sigmoid(gate) * both[:, wide:]).astype(BF)
    out = nn(mixed, fresh[pl.ds(2 * wide, wide)].astype(BF))
    rows = here_ref.shape[0]
    here_ref[...] = out[:rows]
    away_ref[...] = out[rows : 2 * rows]
    send_here_ref[...] = out[2 * rows : 3 * rows].astype(BF)
    send_away_ref[...] = out[3 * rows :].astype(BF)


def per_device(queries, keys, values, segment, rates, fast_one, fast_three, fast_two):
    n = lax.axis_size("tok")
    half, group = n // 2, n // 8
    count, width = queries.shape
    dim = width // FAST_HEADS
    rows, hidden = fast_one.shape
    wide = hidden // 4
    share = wide // group
    tokens = 8 * count
    shard = lax.axis_index("tok")
    me = shard.astype(jnp.int32).reshape(1)

    k_other, *pieces = call(
        functools.partial(first_kernel, half),
        [struct((count, dim), BF)] + [struct((3, rows, wide), BF)] * 4,
        [SM] + [HBM] * 4, [VM] * 5, (me, *in_hbm(keys, fast_one, fast_three, fast_two)),
        [pltpu.SemaphoreType.DMA((13,))])
    kz = swap(k_other, half)
    got = [pieces[0]] + [swap(pieces[k], k) for k in range(1, 4)]
    kv, v_other = call(
        functools.partial(second_kernel, half),
        [struct((2, count, dim), BF), struct((count, dim), BF)],
        [SM] + [HBM] * 2, [VM] * 2, (me, *in_hbm(keys, values)), [pltpu.SemaphoreType.DMA((3,))])
    vz = swap(v_other, half)
    bundle = jnp.stack(got)
    bundles = [bundle] + [swap(bundle, 4 * j) for j in range(1, group)]
    kv_x1 = swap(kv, 2)
    kv_c = swap(kv, 1)
    kv_x1c = swap(kv_x1, 1)
    rate = rates.T[None]
    for offset in (half, 1, 2):
        rate = jnp.concatenate([rate, swap(rate, offset)], 0)
    kx2 = swap(kz, 2)
    kz_c = swap(kz, 1)
    kx2_c = swap(kx2, 1)
    s, e1, e3, w2, wt = call(
      functools.partial(forward_kernel, half, group),
      [struct((tokens, wide), BF), struct((tokens, wide), F32), struct((tokens, wide), F32),
       struct((dim, wide), BF), struct((3, share, dim), F32)],
      [SM] + [VM] * (9 + group), [VM] * 5,
      (me, rate, kv, kv_c, kv_x1, kv_x1c, kz, kz_c, kx2, kx2_c, *bundles),
      [pltpu.VMEM((dim, 2 * wide), BF)], flops=4 * tokens * dim * wide)
    vx2 = swap(vz, 2)
    vz_c = swap(vz, 1)
    vx2_c = swap(vx2, 1)
    grads = call(
      functools.partial(backward_kernel, group),
      [struct((3, share, dim), F32)] + [struct((3, share, dim), BF)] * (group - 1),
      [SM] + [VM] * 16, [VM] * group,
      (me, kv, kv_c, kv_x1, kv_x1c, kz, kz_c, kx2, kx2_c, vz, vz_c, vx2, vx2_c, s, e1, e3, w2),
      [pltpu.VMEM((3 * wide, dim), F32)], flops=8 * tokens * dim * wide)
    sums = [grads[0]] + [swap(grads[j], 4 * j) for j in range(1, group)]
    (fresh,) = call(functools.partial(update_kernel, group), [struct((3, share, dim), BF)],
                    [VM] * (group + 1), [VM], (wt, *sums))

    q_mine, q_other = call(functools.partial(query_kernel, half), [struct((count, dim), BF)] * 2,
                           [SM, HBM], [VM] * 2, (me, *in_hbm(queries)), [pltpu.SemaphoreType.DMA((2,))])
    qz = swap(q_other, half)
    q_c = swap(q_mine, 1)
    qz_c = swap(qz, 1)

    parts = 2 * group
    shares = [fresh] + [swap(fresh, 2 * j) for j in range(1, parts)]
    kind = BF if share % 16 == 0 else F32
    here, away, send_here, send_away = call(
        functools.partial(output_kernel, parts),
        [struct((count, dim), F32)] * 2 + [struct((count, dim), BF)] * 2,
        [VM] * (4 + parts), [VM] * 4, (q_mine, qz, q_c, qz_c, *shares),
        [pltpu.VMEM((3 * parts * share, dim), kind), pltpu.VMEM((4 * count, dim), BF)],
        flops=6 * 4 * count * dim * parts * share)
    away = (away + swap(send_away, 1).astype(F32)).astype(BF)
    away = swap(away, half)
    here = (here + swap(send_here, 1).astype(F32)).astype(BF)
    head = shard // half
    fast_out = jnp.where(head == 0, jnp.concatenate([here, away], 1), jnp.concatenate([away, here], 1))

    chain = [(i, i + 1) for i in range(n - 1)]
    pk = shift(keys, chain)
    pv = shift(values, chain)
    seg_row = segment.reshape(1, count)
    ps = shift(seg_row, chain)
    (attended,) = call(
        functools.partial(attention_kernel, ATT_HEADS), [struct((count, width), BF)],
        [SM] + [VM] * 8, [VM],
        (me, queries, keys, values, pk, pv, segment.reshape(count, 1), seg_row, ps),
        flops=8 * count * count * width)
    return attended, fast_out


def solution(mesh):
    placed = tuple(P(("grp", "tok")) if i == 3 else P(("grp", "tok"), None) for i in range(8))

    return jax.shard_map(
        per_device,
        mesh=mesh,
        in_specs=placed,
        out_specs=(P(("grp", "tok"), None), P(("grp", "tok"), None)),
        check_vma=False,
    )
```

```python
import functools
import math

import jax
import jax.numpy as jnp
from jax import lax
from jax.experimental import pallas as pl
from jax.experimental.pallas import tpu as pltpu
from jax.sharding import PartitionSpec as P


ATT_HEADS = 16
FAST_HEADS = 2
EPS = 1e-06

BF = jnp.bfloat16
F32 = jnp.float32
VM = pl.BlockSpec(memory_space=pltpu.VMEM)
SM = pl.BlockSpec(memory_space=pltpu.SMEM)
HBM = pl.BlockSpec(memory_space=pltpu.HBM)


def struct(shape, dtype):
    return jax.ShapeDtypeStruct(shape, dtype)


def call(body, outs, in_specs, out_specs, args, scratch=(), flops=0, limit=20, alias=None):
    moved = sum(a.size * a.dtype.itemsize for a in args)
    moved += sum(math.prod(o.shape) * jnp.dtype(o.dtype).itemsize for o in outs)
    return pl.pallas_call(
        body,
        out_shape=tuple(outs),
        in_specs=in_specs,
        out_specs=tuple(out_specs),
        scratch_shapes=list(scratch),
        cost_estimate=pl.CostEstimate(flops=flops, bytes_accessed=moved, transcendentals=0),
        compiler_params=pltpu.CompilerParams(vmem_limit_bytes=limit << 20),
        input_output_aliases=alias or {},
    )(*args)


def in_hbm(*arrays):
    return [pltpu.with_memory_space_constraint(a, pltpu.HBM) for a in arrays]


def shift(value, pairs):
    return lax.ppermute(value, "tok", pairs)


def swap(value, offset):
    return shift(value, [(i, i ^ offset) for i in range(lax.axis_size("tok"))])


def nn(a, b):
    return lax.dot_general(a, b, (((1,), (0,)), ((), ())), preferred_element_type=F32)


def nt(a, b):
    return lax.dot_general(a, b, (((1,), (1,)), ((), ())), preferred_element_type=F32)


def tn(a, b):
    return lax.dot_general(a, b, (((0,), (0,)), ((), ())), preferred_element_type=F32)


def run(copies):
    for copy in copies:
        copy.start()
    for copy in copies:
        copy.wait()


def first_kernel(half, me_ref, k_ref, w1_ref, w3_ref, w2_ref, ko_ref, *rest):
    pieces, sems = rest[:4], rest[4]
    me = me_ref[0]
    dim = ko_ref.shape[1]
    other = pl.ds(pl.multiple_of((1 - me // half) * dim, dim), dim)
    copies = [pltpu.make_async_copy(k_ref.at[:, other], ko_ref, sems.at[0])]
    wide = pieces[0].shape[2]
    for k in range(4):
        cols = pl.ds(pl.multiple_of((me % 4 ^ k) * wide, wide), wide)
        for m, w_ref in enumerate((w1_ref, w3_ref, w2_ref)):
            copies.append(pltpu.make_async_copy(w_ref.at[:, cols], pieces[k].at[m], sems.at[1 + 3 * k + m]))
    run(copies)


def second_kernel(half, me_ref, k_ref, v_ref, kv_ref, va_ref, vb_ref, sems):
    head = me_ref[0] // half
    rows, dim = va_ref.shape
    mine = pl.ds(pl.multiple_of(head * dim, dim), dim)
    other = pl.ds(pl.multiple_of((1 - head) * dim, dim), dim)
    run([
        pltpu.make_async_copy(v_ref.at[pl.ds(0, rows), other], va_ref, sems.at[0]),
        pltpu.make_async_copy(v_ref.at[pl.ds(rows, rows), other], vb_ref, sems.at[3]),
        pltpu.make_async_copy(k_ref.at[:, mine], kv_ref.at[0], sems.at[1]),
        pltpu.make_async_copy(v_ref.at[:, mine], kv_ref.at[1], sems.at[2]),
    ])


def query_kernel(half, me_ref, q_ref, qm_ref, qo_ref, sems):
    head = me_ref[0] // half
    dim = qm_ref.shape[1]
    run([
        pltpu.make_async_copy(q_ref.at[:, pl.ds(pl.multiple_of((1 - head) * dim, dim), dim)], qo_ref, sems.at[0]),
        pltpu.make_async_copy(q_ref.at[:, pl.ds(pl.multiple_of(head * dim, dim), dim)], qm_ref, sems.at[1]),
    ])


def stack_kernel(k_ref, v_ref, out_ref, sems):
    run([
        pltpu.make_async_copy(k_ref, out_ref.at[0], sems.at[0]),
        pltpu.make_async_copy(v_ref, out_ref.at[1], sems.at[1]),
    ])


def relay_kernel(me_ref, own_ref, far_ref, out_ref):
    last = me_ref[0] % 4 == 3

    @pl.when(last)
    def _():
        out_ref[...] = far_ref[...]

    @pl.when(jnp.logical_not(last))
    def _():
        out_ref[...] = own_ref[...]


def sum_kernel(own_ref, far_ref, out_ref):
    out_ref[...] = (own_ref[...] + far_ref[...].astype(F32)).astype(BF)


def near_kernel(half, me_ref, own_ref, far_ref, out_ref, held, sems):
    held[...] = (own_ref[...] + far_ref[...].astype(F32)).astype(BF)
    dim = held.shape[1]
    mine = pl.ds(pl.multiple_of(me_ref[0] // half * dim, dim), dim)
    run([pltpu.make_async_copy(held, out_ref.at[:, mine], sems.at[0])])


def away_kernel(half, me_ref, away_ref, in_ref, out_ref, sems):
    dim = away_ref.shape[1]
    other = pl.ds(pl.multiple_of((1 - me_ref[0] // half) * dim, dim), dim)
    run([pltpu.make_async_copy(away_ref, out_ref.at[:, other], sems.at[0])])


def attention_kernel(heads, half, me_ref, q_ref, kv_ref, before_ref, cross_ref, seg_ref, ps_ref, o_ref):
    count, width = q_ref.shape
    dim = width // heads
    scale = 1.0 / math.sqrt(dim)
    rows = lax.broadcasted_iota(jnp.int32, (count, count), 0)
    cols = lax.broadcasted_iota(jnp.int32, (count, count), 1)
    own = seg_ref[...]
    column = jnp.broadcast_to(own.astype(F32), (8, count)).T[:, 0:1].astype(jnp.int32)
    here = (cols <= rows) & (column == own)
    before = (cols > rows) & (column == ps_ref[...]) & (me_ref[0] > 0)
    cross = me_ref[0] == half
    for h in range(heads):
        part = slice(h * dim, (h + 1) * dim)
        q = q_ref[:, part]
        pk = jnp.where(cross, cross_ref[0, :, part], before_ref[0, :, part])
        pv = jnp.where(cross, cross_ref[1, :, part], before_ref[1, :, part])
        s0 = jnp.where(before, nt(q, pk) * scale, F32(-1e30))
        s1 = jnp.where(here, nt(q, kv_ref[0, :, part]) * scale, F32(-1e30))
        top = jnp.maximum(jnp.max(s0, axis=1, keepdims=True), jnp.max(s1, axis=1, keepdims=True))
        e0 = jnp.where(before, jnp.exp(s0 - top), F32(0.0))
        e1 = jnp.where(here, jnp.exp(s1 - top), F32(0.0))
        total = jnp.sum(e0, axis=1, keepdims=True) + jnp.sum(e1, axis=1, keepdims=True)
        out = nn((e0 / total).astype(BF), pv) + nn((e1 / total).astype(BF), kv_ref[1, :, part])
        o_ref[:, part] = out.astype(BF)


def rows_of(*parts):
    return jnp.concatenate(parts, 0)


def forward_kernel(half, group, me_ref, r_ref, *refs):
    own, own_c, x1, x1_c, z, z_c, x2, x2_c = refs[:8]
    bundles = refs[8 : 8 + group]
    s_ref, e1_ref, e3_ref, w2_ref, wt_ref, w13 = refs[8 + group :]
    me = me_ref[0]
    quarter, place = me % 4, (me // 4) % group
    wide = w2_ref.shape[1]
    rows = bundles[0].shape[2]
    for j in range(group):
        for k in range(4):
            at = pl.ds(pl.multiple_of(((place ^ j) * 4 + (quarter ^ k)) * rows, rows), rows)
            w13[at, 0:wide] = bundles[j][k, 0]
            w13[at, wide : 2 * wide] = bundles[j][k, 1]
            w2_ref[at, :] = bundles[j][k, 2]
    share = wt_ref.shape[1]
    pick = lax.broadcasted_iota(jnp.int32, (share, wide), 1) == (
        lax.broadcasted_iota(jnp.int32, (share, wide), 0) + place * share
    )
    pick = pick.astype(F32).astype(BF)
    wt_ref[0] = nt(pick, w13[:, 0:wide])
    wt_ref[1] = nt(pick, w13[:, wide : 2 * wide])
    wt_ref[2] = nt(pick, w2_ref[...])
    rate = -jnp.where(me // half == 0, r_ref[:, 0, :], r_ref[:, 1, :]).T
    held = rows_of(own[0], own_c[0], x1[0], x1_c[0], z[...], z_c[...], x2[...], x2_c[...])
    both = nn(held, w13[...])
    count = held.shape[0] // 8
    for i in range(8):
        part = slice(i * count, (i + 1) * count)
        a1, a3 = both[part, :wide], both[part, wide:]
        at = (i & 1) + 2 * (i >> 2) + 4 * (i >> 1 & 1)
        r = rate[:, at : at + 1]
        sig = jax.nn.sigmoid(a1)
        gate = r * a1 * sig
        s_ref[part, :] = (gate * a3).astype(BF)
        e1_ref[part, :] = r * a3 * sig * (1.0 + a1 * (1.0 - sig))
        e3_ref[part, :] = gate


def backward_kernel(group, me_ref, *refs):
    own, own_c, x1, x1_c = refs[:4]
    kz, kz_c, kx2, kx2_c = refs[4:8]
    far = refs[8:16]
    s_ref, e1_ref, e3_ref, w2_ref = refs[16:20]
    outs = refs[20 : 20 + group]
    (grads,) = refs[20 + group :]
    keys = rows_of(own[0], own_c[0], x1[0], x1_c[0], kz[...], kz_c[...], kx2[...], kx2_c[...])
    values = rows_of(own[1], own_c[1], x1[1], x1_c[1], *[v[...] for v in far])
    place = (me_ref[0] // 4) % group
    wide = w2_ref.shape[1]
    back = nn(values, w2_ref[...])
    delta = jnp.concatenate([(back * e1_ref[...]).astype(BF), (back * e3_ref[...]).astype(BF)], 1)
    grads[pl.ds(2 * wide, wide)] = tn(s_ref[...], values)
    grads[pl.ds(0, 2 * wide)] = tn(delta, keys)
    share = outs[0].shape[1]
    for j in range(group):
        for m in range(3):
            at = pl.ds(pl.multiple_of(m * wide + (place ^ j) * share, share), share)
            outs[j][m] = grads[at, :].astype(outs[j].dtype)


def update_kernel(group, wt_ref, *refs):
    parts, outs = refs[:group], refs[group:]
    grad = parts[0][...].astype(F32)
    for part in parts[1:]:
        grad = grad + part[...].astype(F32)
    weight = wt_ref[...]
    fresh = weight - grad
    old_len = jnp.sqrt(jnp.sum(weight * weight, axis=2, keepdims=True))
    new_len = jnp.sqrt(jnp.sum(fresh * fresh, axis=2, keepdims=True) + EPS)
    fresh = (fresh * (old_len / new_len)).astype(BF)
    for m, out_ref in enumerate(outs):
        out_ref[...] = fresh[m]


def output_kernel(orders, own, far, *refs):
    shares = refs[:6]
    out_ref, send_ref, held, fresh, sems = refs[6:]
    rows = own.shape[0]
    copies = [
        pltpu.make_async_copy(own, held.at[pl.ds(0, rows)], sems.at[0]),
        pltpu.make_async_copy(far, held.at[pl.ds(rows, rows)], sems.at[1]),
    ]
    for copy in copies:
        copy.start()
    parts = len(orders[0])
    share = 2 * shares[0].shape[0] // parts
    wide = share * parts
    for m, order in enumerate(orders):
        both = [shares[2 * m + side][...].astype(fresh.dtype) for side in range(2)]
        for place, i in enumerate(order):
            side, at = divmod(place, parts // 2)
            fresh[pl.ds(m * wide + i * share, share)] = both[side][at * share : (at + 1) * share]
    for copy in copies:
        copy.wait()
    both = nt(held[...], fresh[pl.ds(0, 2 * wide)].astype(BF))
    gate = both[:, :wide]
    mixed = (gate * jax.nn.sigmoid(gate) * both[:, wide:]).astype(BF)
    out = nn(mixed, fresh[pl.ds(2 * wide, wide)].astype(BF))
    out_ref[...] = out[:rows]
    send_ref[...] = out[rows:].astype(BF)


def gather_routes(parts):
    bits = [1 << b for b in range(parts.bit_length() - 1)]
    return [bits[m % len(bits) :] + bits[: m % len(bits)] for m in range(3)]


def route_order(route):
    order = [0]
    for bit in route:
        order = order + [i ^ bit for i in order]
    return order


def per_device(queries, keys, values, segment, rates, fast_one, fast_three, fast_two):
    n = lax.axis_size("tok")
    half, group = n // 2, n // 8
    count, width = queries.shape
    dim = width // FAST_HEADS
    rows, hidden = fast_one.shape
    wide = hidden // 4
    share = wide // group
    tokens = 8 * count
    shard = lax.axis_index("tok")
    me = shard.astype(jnp.int32).reshape(1)

    k_other, *pieces = call(
        functools.partial(first_kernel, half),
        [struct((count, dim), BF)] + [struct((3, rows, wide), BF)] * 4, [SM] + [HBM] * 4, [VM] * 5,
        (me, *in_hbm(keys, fast_one, fast_three, fast_two)), [pltpu.SemaphoreType.DMA((13,))])
    kz = swap(k_other, half)
    got = [pieces[0]] + [swap(pieces[k], k) for k in range(1, 4)]
    kv, *v_other = call(
      functools.partial(second_kernel, half),
      [struct((2, count, dim), BF)] + [struct((count // 2, dim), BF)] * 2,
      [SM] + [HBM] * 2, [VM] * 3, (me, *in_hbm(keys, values)), [pltpu.SemaphoreType.DMA((4,))])
    vz = [swap(v, half) for v in v_other]
    bundle = jnp.stack(got)
    bundles = [bundle] + [swap(bundle, 4 * j) for j in range(1, group)]
    kv_x1 = swap(kv, 2)
    kv_c = swap(kv, 1)
    kv_x1c = swap(kv_x1, 1)
    rate = rates.T[None]
    for offset in (1, half, 2):
        rate = jnp.concatenate([rate, swap(rate, offset)], 0)
    kx2 = swap(kz, 2)
    kz_c = swap(kz, 1)
    kx2_c = swap(kx2, 1)
    s, e1, e3, w2, wt = call(
      functools.partial(forward_kernel, half, group),
      [struct((tokens, wide), BF), struct((tokens, wide), F32), struct((tokens, wide), F32),
       struct((dim, wide), BF), struct((3, share, dim), F32)],
      [SM] + [VM] * (9 + group), [VM] * 5,
      (me, rate, kv, kv_c, kv_x1, kv_x1c, kz, kz_c, kx2, kx2_c, *bundles),
      [pltpu.VMEM((dim, 2 * wide), BF)], flops=4 * tokens * dim * wide)
    vx2 = [swap(v, 2) for v in vz]
    vz_c = [swap(v, 1) for v in vz]
    vx2_c = [swap(v, 1) for v in vx2]
    grads = call(
      functools.partial(backward_kernel, group),
      [struct((3, share, dim), F32)] + [struct((3, share, dim), BF)] * (group - 1),
      [SM] + [VM] * 20, [VM] * group,
      (me, kv, kv_c, kv_x1, kv_x1c, kz, kz_c, kx2, kx2_c, *vz, *vz_c, *vx2, *vx2_c, s, e1, e3, w2),
      [pltpu.VMEM((3 * wide, dim), F32)], flops=8 * tokens * dim * wide)
    sums = [grads[0]] + [swap(grads[j], 4 * j) for j in range(1, group)]
    fresh = call(functools.partial(update_kernel, group), [struct((share, dim), BF)] * 3,
               [VM] * (group + 1), [VM] * 3, (wt, *sums))

    q_mine, q_other = call(functools.partial(query_kernel, half), [struct((count, dim), BF)] * 2,
                         [SM, HBM], [VM] * 2, (me, *in_hbm(queries)), [pltpu.SemaphoreType.DMA((2,))])
    qz = swap(q_other, half)
    q_c = swap(q_mine, 1)
    qz_c = swap(qz, 1)

    parts = 2 * group
    routes = gather_routes(parts)
    shares = []
    for m, route in enumerate(routes):
        whole = fresh[m]
        for step, bit in enumerate(route):
            got = swap(whole, 2 * bit)
            if step < len(route) - 1:
                whole = jnp.concatenate([whole, got], 0)
        shares += [whole, got]
    orders = [route_order(route) for route in routes]
    kind = BF if share % 16 == 0 else F32

    def output(*tokens):
        return call(
            functools.partial(output_kernel, orders),
            [struct((count, dim), F32), struct((count, dim), BF)],
            [VM] * 8, [VM] * 2, (*tokens, *shares),
            [pltpu.VMEM((2 * count, dim), BF), pltpu.VMEM((3 * parts * share, dim), kind), pltpu.SemaphoreType.DMA((2,))],
            flops=6 * 2 * count * dim * parts * share)

    away, send_away = output(qz, qz_c)
    here, send_here = output(q_mine, q_c)

    def named(*args, **more):
        return call(*args, **more)[0]

    away = named(sum_kernel, [struct((count, dim), BF)], [VM] * 2, [VM], (away, swap(send_away, 1)))
    away = swap(away, half)
    fast_out = named(functools.partial(near_kernel, half), [struct((count, width), BF)], [SM, VM, VM], [HBM],
                     (me, here, swap(send_here, 1)),
                     scratch=[pltpu.VMEM((count, dim), BF), pltpu.SemaphoreType.DMA((1,))])
    fast_out = named(functools.partial(away_kernel, half), [struct((count, width), BF)], [SM, VM, HBM], [HBM],
                     (me, away, fast_out), scratch=[pltpu.SemaphoreType.DMA((1,))], alias={2: 0})

    ring = [(i, i + 1) for i in range(n) if i % 4 < 3] + [(i, i - 3) for i in range(7, n, 4) if i != half + 3]
    relay = [(i, i + 4) for i in range(3, n - 4, 4) if i != half - 1]
    full = named(stack_kernel, [struct((2, count, width), BF)], [HBM] * 2, [VM], tuple(in_hbm(keys, values)),
                 scratch=[pltpu.SemaphoreType.DMA((2,))])
    passed = named(relay_kernel, [struct((2, count, width), BF)], [SM, VM, VM], [VM],
                   (me, full, shift(full, relay)))
    before, cross = shift(passed, ring), shift(full, [(half - 1, half)])
    seg_row = segment.reshape(1, count)
    ps = shift(seg_row, [(i, i + 1) for i in range(n - 1)])
    attended = named(
        functools.partial(attention_kernel, ATT_HEADS, half), [struct((count, width), BF)], [SM] + [VM] * 6, [VM],
        (me, queries, full, before, cross, seg_row, ps), flops=8 * count * count * width)
    return attended, fast_out


def solution(mesh):
    placed = tuple(P(("grp", "tok")) if i == 3 else P(("grp", "tok"), None) for i in range(8))

    return jax.shard_map(
        per_device,
        mesh=mesh,
        in_specs=placed,
        out_specs=(P(("grp", "tok"), None), P(("grp", "tok"), None)),
        check_vma=False,
    )
```
